32 devices in a mesh: grp: 2 (over core), aux: 8 (over z, x), tr: 2 (over y).
Axes of the slice: x: 2, y: 2, z: 4, core: 2. Of those that a mesh axis runs over, the one named last changes fastest.
Arguments:
- trial_vectors: float32 [64, 8, 512], P('aux', None, 'tr'), may hold values from -6 to 6
- energy_val: float32 [64], P('aux'), may hold values from -1 to -0.2
- energy_cond: float32 [512], P('tr'), may hold values from 0.2 to 2
- coef_occ: bfloat16 [512, 64, 64], P('aux'), may hold values from -0.75 to 0.75
- coef_virt: bfloat16 [512, 512, 512], P('aux', 'tr'), may hold values from -0.01171875 to 0.01171875
- pair_coef: bfloat16 [64, 512, 512], P('aux', 'tr'), may hold values from -0.03125 to 0.03125
- live_aux: int32 [8], P('aux'), may hold values from 16 to 64, as said below
Outputs:
- applied: float32 [64, 8, 512], P('aux', None, 'tr')
- intersection: float32 [8, 8], replicated
The draws below stay inside these ranges and needn't reach their ends.
Inputs may be any that keep to these rules, and one draw needn't show every extreme that they name: `live_aux`: equals 64 on at least one shard.
All inputs are finite; a program needn't handle non-finite values.
Results may differ from the reference program's by a relative error of at most 0.0048.
Values may be sent and summed in bfloat16 or wider, within the bound.
A program may use at most 64 MiB of HBM per device.

```python
import jax
import jax.numpy as jnp
from jax import lax

V = 64
C = 512
K = 8
PD = 64
NSHARD = 8
NAUX = 512


def draw_live_aux(key, part):
    counts = jax.random.randint(jax.random.fold_in(key, 17), (NSHARD,), PD // 4, PD + 1)
    chosen = jax.random.randint(jax.random.fold_in(key, 29), (), 0, NSHARD)
    return counts.at[chosen].set(PD).astype(jnp.int32)


def block_scale(rng, dims, cuts, least, top_value):
    def one(dim, shards_of):
        draws = jax.random.uniform(jax.random.fold_in(jax.random.fold_in(rng, 6), dim), (shards_of,), jnp.float32, least / len(cuts), top_value / len(cuts))
        return jnp.repeat(jnp.exp(draws), dims[dim] // shards_of).reshape((-1,) + (1,) * (len(dims) - dim - 1))

    loudness = one(*cuts[0])
    for cut in cuts[1:]:
        loudness = loudness * one(*cut)
    return loudness


def bell_draw(key, shape, deviation, bound, cuts=(), held_as=jnp.bfloat16):
    loudness = block_scale(key, shape, cuts, -0.22, 0.18) if cuts else 1.0
    drawn = jax.random.normal(key, shape, jnp.float32) * deviation * loudness
    return jnp.minimum(jnp.maximum(drawn, -bound), bound).astype(held_as)


def setup_inputs(seed: int = 0) -> dict:
    streams_of = jax.random.split(jax.random.key(seed), 8)
    trial_vectors = bell_draw(streams_of[0], (V, K, C), 1.0, 6.0, ((0, 8), (2, 2)), jnp.float32)
    energy_val = jnp.clip(-1.0 + 0.8 * jax.random.uniform(streams_of[1], (V,), jnp.float32) ** block_scale(streams_of[1], (V,), ((0, 8),), -0.2, 0.2), -1.0, -0.2)
    energy_cond = jnp.clip(0.2 + 1.8 * jax.random.uniform(streams_of[2], (C,), jnp.float32) ** block_scale(streams_of[2], (C,), ((0, 2),), -0.2, 0.2), 0.2, 2.0)
    coef_occ = bell_draw(streams_of[3], (NAUX, V, V), V ** -0.5, 0.75, ((0, 8),))
    coef_virt = bell_draw(streams_of[4], (NAUX, C, C), (C * NAUX) ** -0.5, 0.01171875, ((0, 8), (1, 2)))
    pair_coef = bell_draw(streams_of[5], (V, C, NAUX), (V * C) ** -0.5, 0.03125, ((0, 8), (1, 2)))
    live_aux = draw_live_aux(jax.random.fold_in(streams_of[7], 71), 0)
    return dict(trial_vectors=trial_vectors, energy_val=energy_val, energy_cond=energy_cond, coef_occ=coef_occ, coef_virt=coef_virt, pair_coef=pair_coef, live_aux=live_aux)


def apply_hamiltonian(vectors, energy_gap, coef_occ, coef_virt, pair_coef, live_aux):
    rounded = vectors.astype(jnp.bfloat16)
    rounded_wide = rounded.astype(jnp.float32)

    def one_shard(running, shard_index):
        block_occ = lax.dynamic_slice_in_dim(coef_occ, shard_index * PD, PD, 0).astype(jnp.float32)
        block_virt = lax.dynamic_slice_in_dim(coef_virt, shard_index * PD, PD, 0).astype(jnp.float32)
        keep_mask = (jnp.arange(PD, dtype=jnp.int32) < live_aux[shard_index]).astype(jnp.float32)
        blended = jnp.einsum('puv,vkc->pukc', block_occ, rounded_wide)
        blended = (blended * keep_mask[:, None, None, None]).astype(jnp.bfloat16)
        running = running + jnp.einsum('pukc,pcd->ukd', blended.astype(jnp.float32), block_virt)
        return running, None

    zero_term = jnp.zeros((V, K, C), jnp.float32)
    direct_term, _ = lax.scan(one_shard, zero_term, jnp.arange(NSHARD, dtype=jnp.int32))
    pair_wide = pair_coef.astype(jnp.float32)
    projection = jnp.einsum('vcp,vkc->kp', pair_wide, rounded_wide)
    projection_b = projection.astype(jnp.bfloat16)
    exchange_term = jnp.einsum('vcp,kp->vkc', pair_wide, projection_b.astype(jnp.float32))
    return energy_gap[:, None, :] * vectors + direct_term + exchange_term


def reference(trial_vectors, energy_val, energy_cond, coef_occ, coef_virt, pair_coef, live_aux):
    energy_gap = energy_cond[None, :] - energy_val[:, None]
    applied_first = apply_hamiltonian(trial_vectors, energy_gap, coef_occ, coef_virt, pair_coef, live_aux)
    intersection = jnp.einsum('vkc,vjc->kj', trial_vectors, applied_first, precision=lax.Precision.HIGHEST) / (V * C)
    residual = applied_first - jnp.einsum('vkc,kj->vjc', trial_vectors, intersection, precision=lax.Precision.HIGHEST)
    correction = residual / energy_gap[:, None, :]
    applied = apply_hamiltonian(correction, energy_gap, coef_occ, coef_virt, pair_coef, live_aux)
    return applied, intersection
```

```python
import functools

import jax
import jax.numpy as jnp
from jax import lax
from jax.experimental import pallas as pl
from jax.experimental.pallas import tpu as pltpu
from jax.sharding import PartitionSpec as P

F32 = jnp.float32
BF16 = jnp.bfloat16
MESH = pl.DeviceIdType.MESH


def kernel(
    naux, ntr, chunk,
    live_ref, trial_ref, val_ref, cond_ref, occ_hbm, virt_hbm, pair_hbm,
    out_ref, inter_ref,
    occ, virt, pair, blended, acc, wide, mixed,
    block_send, block_recv, proj_send, proj_recv, tr_send, tr_recv,
    sum_send, sum_recv, dots_send, dots_recv, core_recv, final_send, final_recv,
    load_sem, virt_sem, block_ssem, block_rsem, proj_ssem, proj_rsem,
    tr_ssem, tr_rsem, sum_ssem, sum_rsem, dots_ssem, dots_rsem, core_ssem, core_rsem,
):
    g = lax.axis_index("grp")
    a = lax.axis_index("aux")
    t = lax.axis_index("tr")
    vectors, own_val, cond = trial_ref.shape
    half = vectors // 2
    slots, val, _ = occ.shape
    chunks = slots // chunk
    other_t = lax.rem(t + 1, ntr)
    own_cols = pl.ds(pl.multiple_of(t * cond, cond), cond)
    other_cols = pl.ds(pl.multiple_of(other_t * cond, cond), cond)

    occ_copy = pltpu.make_async_copy(occ_hbm, occ, load_sem.at[0])
    pair_copy = pltpu.make_async_copy(pair_hbm, pair, load_sem.at[1])
    occ_copy.start()
    pair_copy.start()

    def virt_copy(i):
        part = pl.ds(i * chunk, chunk)
        return pltpu.make_async_copy(virt_hbm.at[part], virt.at[part], virt_sem.at[i])

    for i in range(chunks):
        virt_copy(i).start()

    everyone = [(da, dt) for da in range(naux) for dt in range(ntr) if (da, dt) != (0, 0)]

    def peer(da, dt):
        return {"aux": lax.rem(a + da, naux), "tr": lax.rem(t + dt, ntr)}

    barrier = pltpu.get_barrier_semaphore()
    for da, dt in everyone:
        pl.semaphore_signal(barrier, inc=1, device_id=peer(da, dt), device_id_type=MESH)
    pl.semaphore_signal(barrier, inc=1, device_id={"grp": 1 - g}, device_id_type=MESH)

    gap = cond_ref[...] - val_ref[...]

    def to_all(it, send, recv, ssem, rsem):
        copies = []
        for da, dt in everyone:
            n = da * ntr + dt
            copies.append(pltpu.make_async_remote_copy(
                src_ref=send.at[it], dst_ref=recv.at[it, n],
                send_sem=ssem.at[it, n], recv_sem=rsem.at[it, n],
                device_id=peer(da, dt), device_id_type=MESH))
        return copies

    def apply(it, x):
        block = jnp.concatenate(x, axis=1).astype(BF16)
        block_send[it] = block
        block_recv[it, a] = block
        if it == 0:
            pl.semaphore_wait(barrier, len(everyone) + 1)
        gathers = []
        for d in range(1, naux):
            copy = pltpu.make_async_remote_copy(
                src_ref=block_send.at[it], dst_ref=block_recv.at[it, a],
                send_sem=block_ssem.at[it, d], recv_sem=block_rsem.at[it, d],
                device_id=peer(d, 0), device_id_type=MESH)
            copy.start()
            gathers.append(copy)

        if it == 0:
            pair_copy.wait()
        for k in range(half):
            mixed[:, k, :] = x[k]
        proj = jnp.zeros((half, pair.shape[2]), F32)
        for v in range(own_val):
            proj += jnp.dot(mixed[v].astype(BF16), pair[v], preferred_element_type=F32)
        proj_send[it] = proj
        projections = to_all(it, proj_send, proj_recv, proj_ssem, proj_rsem)
        for copy in projections:
            copy.start()

        if it == 0:
            occ_copy.wait()
            live = live_ref[0, 0]

            @pl.loop(0, slots)
            def _(p):
                keep = (p < live).astype(F32)
                occ[p] = (occ[p].astype(F32) * keep).astype(BF16)

        for copy in gathers:
            copy.wait_recv()
        for s in range(naux):
            wide[pl.ds(s * own_val, own_val), :] = block_recv[it, s].astype(F32)
        gathered = [wide[:, k * cond:(k + 1) * cond].astype(BF16) for k in range(half)]
        acc[...] = jnp.zeros_like(acc)

        @pl.loop(0, chunks)
        def _(i):
            if it == 0:
                virt_copy(i).wait()
            part = pl.ds(i * chunk, chunk)
            occ_part = occ[part].reshape(chunk * val, val)
            for k in range(half):
                b = jnp.dot(occ_part, gathered[k], preferred_element_type=F32).astype(BF16)
                for q in range(chunk):
                    blended[i, k * val:(k + 1) * val, q * cond:(q + 1) * cond] = b[q * val:(q + 1) * val]
            acc[...] += jnp.dot(
                blended[i], virt[part, :, other_cols].reshape(chunk * cond, cond),
                preferred_element_type=F32)

        tr_send[it] = acc[...].astype(BF16)
        tr_copy = pltpu.make_async_remote_copy(
            src_ref=tr_send.at[it], dst_ref=tr_recv.at[it],
            send_sem=tr_ssem.at[it], recv_sem=tr_rsem.at[it],
            device_id=peer(0, 1), device_id_type=MESH)
        tr_copy.start()
        acc[...] = jnp.zeros_like(acc)

        @pl.loop(0, chunks)
        def _(i):
            part = pl.ds(i * chunk, chunk)
            acc[...] += jnp.dot(
                blended[i], virt[part, :, own_cols].reshape(chunk * cond, cond),
                preferred_element_type=F32)

        tr_copy.wait_recv()
        acc[...] += tr_recv[it].astype(F32)
        for s in range(naux):
            for k in range(half):
                row = k * val + s * own_val
                sum_send[it, s, :, k * cond:(k + 1) * cond] = acc[row:row + own_val, :].astype(BF16)
        sums = []
        for d in range(1, naux):
            copy = pltpu.make_async_remote_copy(
                src_ref=sum_send.at[it, lax.rem(a + d, naux)], dst_ref=sum_recv.at[it, d],
                send_sem=sum_ssem.at[it, d], recv_sem=sum_rsem.at[it, d],
                device_id=peer(d, 0), device_id_type=MESH)
            copy.start()
            sums.append(copy)

        for copy in projections:
            copy.wait_recv()
        proj = proj_send[it]
        for da, dt in everyone:
            proj += proj_recv[it, da * ntr + dt]
        proj_b = proj.astype(BF16)
        for v in range(own_val):
            mixed[v] = lax.dot_general(
                proj_b, pair[v], (((1,), (1,)), ((), ())), preferred_element_type=F32)
        total = sum_send[it, a].astype(F32)
        for copy in sums:
            copy.wait_recv()
        for d in range(1, naux):
            total += sum_recv[it, d].astype(F32)
        result = []
        for k in range(half):
            result.append(gap * x[k] + total[:, k * cond:(k + 1) * cond] + mixed[:, k, :])
        for copy in gathers + projections + sums + [tr_copy]:
            copy.wait_send()
        return result

    first = apply(0, [trial_ref[g * half + k] for k in range(half)])

    trial = trial_ref[...]
    lanes = lax.broadcasted_iota(jnp.int32, (vectors, 128), 1)
    partial = jnp.zeros((vectors, 128), F32)
    for j in range(half):
        lanewise = jnp.sum(trial * first[j][None], axis=1)
        column = jnp.sum(lanewise, axis=1, keepdims=True)
        partial += jnp.where(lanes == g * half + j, column, 0.0)
    dots_send[0] = partial
    dots = to_all(0, dots_send, dots_recv, dots_ssem, dots_rsem)
    for copy in dots:
        copy.start()
    for copy in dots:
        copy.wait()
    by_tile = dots_recv[0, 0 + 1]
    for da, dt in everyone[1:]:
        by_tile += dots_recv[0, da * ntr + dt]
    inter = (by_tile + partial) / (naux * own_val * ntr * cond)
    dots_send[1] = inter
    core_dots = pltpu.make_async_remote_copy(
        src_ref=dots_send.at[1], dst_ref=core_recv,
        send_sem=core_ssem.at[0], recv_sem=core_rsem.at[0],
        device_id={"grp": 1 - g}, device_id_type=MESH)
    core_dots.start()

    correction = []
    for j in range(half):
        column = jnp.sum(jnp.where(lanes == g * half + j, inter, 0.0), axis=1, keepdims=True)
        fitted = trial_ref[0] * column[0:1, :]
        for k in range(1, vectors):
            fitted += trial_ref[k] * column[k:k + 1, :]
        correction.append((first[j] - fitted) / gap)

    second = apply(1, correction)
    for k in range(half):
        final_send[k] = second[k]
        out_ref[g * half + k] = second[k]
    final_copy = pltpu.make_async_remote_copy(
        src_ref=final_send, dst_ref=final_recv,
        send_sem=core_ssem.at[1], recv_sem=core_rsem.at[1],
        device_id={"grp": 1 - g}, device_id_type=MESH)
    final_copy.start()
    core_dots.wait()
    inter_ref[...] = (dots_send[1] + core_recv[...])[:, :vectors]
    final_copy.wait()
    for k in range(half):
        out_ref[(1 - g) * half + k] = final_recv[k]


def body(naux, ntr, trial_vectors, energy_val, energy_cond, coef_occ, coef_virt, pair_coef, live_aux):
    own_val, vectors, cond = trial_vectors.shape
    slots, val, _ = coef_occ.shape
    naux_all = pair_coef.shape[2]
    half = vectors // 2
    chunk = 8
    peers = naux * ntr
    vmem = pl.BlockSpec(memory_space=pltpu.VMEM)
    hbm = pl.BlockSpec(memory_space=pl.ANY)
    dma = pltpu.SemaphoreType.DMA
    scratch = [
        pltpu.VMEM(coef_occ.shape, BF16),
        pltpu.VMEM(coef_virt.shape, BF16),
        pltpu.VMEM(pair_coef.shape, BF16),
        pltpu.VMEM((slots // chunk, half * val, chunk * cond), BF16),
        pltpu.VMEM((half * val, cond), F32),
        pltpu.VMEM((val, half * cond), F32),
        pltpu.VMEM((own_val, half, cond), F32),
        pltpu.VMEM((2, own_val, half * cond), BF16),
        pltpu.VMEM((2, naux, own_val, half * cond), BF16),
        pltpu.VMEM((2, half, naux_all), F32),
        pltpu.VMEM((2, peers, half, naux_all), F32),
        pltpu.VMEM((2, half * val, cond), BF16),
        pltpu.VMEM((2, half * val, cond), BF16),
        pltpu.VMEM((2, naux, own_val, half * cond), BF16),
        pltpu.VMEM((2, naux, own_val, half * cond), BF16),
        pltpu.VMEM((2, vectors, 128), F32),
        pltpu.VMEM((1, peers, vectors, 128), F32),
        pltpu.VMEM((vectors, 128), F32),
        pltpu.VMEM((half, own_val, cond), F32),
        pltpu.VMEM((half, own_val, cond), F32),
        dma((2,)), dma((slots // chunk,)),
        dma((2, naux)), dma((2, naux)),
        dma((2, peers)), dma((2, peers)),
        dma((2,)), dma((2,)),
        dma((2, naux)), dma((2, naux)),
        dma((1, peers)), dma((1, peers)),
        dma((2,)), dma((2,)),
    ]
    applied, intersection = pl.pallas_call(
        functools.partial(kernel, naux, ntr, chunk),
        out_shape=(
            jax.ShapeDtypeStruct((vectors, own_val, cond), F32),
            jax.ShapeDtypeStruct((vectors, vectors), F32),
        ),
        in_specs=[pl.BlockSpec(memory_space=pltpu.SMEM), vmem, vmem, vmem, hbm, hbm, hbm],
        out_specs=(vmem, vmem),
        scratch_shapes=scratch,
        compiler_params=pltpu.CompilerParams(
            collective_id=0, has_side_effects=True, vmem_limit_bytes=56 * 1024 * 1024
        ),
    )(
        live_aux.reshape(1, 1), trial_vectors.transpose(1, 0, 2), energy_val.reshape(-1, 1),
        energy_cond.reshape(1, -1), coef_occ, coef_virt, pair_coef,
    )
    return applied.transpose(1, 0, 2), intersection


def solution(mesh):
    in_specs = (
        P("aux", None, "tr"),
        P("aux"),
        P("tr"),
        P("aux", None, None),
        P("aux", "tr", None),
        P("aux", "tr", None),
        P("aux"),
    )
    out_specs = (P("aux", None, "tr"), P())
    sizes = (mesh.shape["aux"], mesh.shape["tr"])
    return jax.shard_map(
        functools.partial(body, *sizes), mesh=mesh, in_specs=in_specs, out_specs=out_specs, check_vma=False
    )
```

```python
import functools

import jax
import jax.numpy as jnp
from jax import lax
from jax.experimental import pallas as pl
from jax.experimental.pallas import tpu as pltpu
from jax.sharding import PartitionSpec as P

F32 = jnp.float32
BF16 = jnp.bfloat16
GROUPS = 1
MESH = pl.DeviceIdType.MESH


def kernel(
    naux, ntr, groups,
    live_ref, trial_ref, val_ref, cond_ref, occ_hbm, virt_hbm, pair_hbm,
    out_ref, inter_ref,
    occ, virt, pair, blended, acc, wide, mixed, trial_k,
    block_send, block_recv, proj_send, proj_recv, tr_send, tr_recv,
    sum_send, sum_recv, dots_send, dots_recv, core_recv, final_send, final_recv,
    load_sem, block_ssem, block_rsem, proj_ssem, proj_rsem,
    tr_ssem, tr_rsem, sum_ssem, sum_rsem, dots_ssem, dots_rsem, core_ssem, core_rsem,
):
    g = lax.axis_index("grp")
    a = lax.axis_index("aux")
    t = lax.axis_index("tr")
    own_val, vectors, cond = trial_ref.shape
    half = vectors // 2
    size = half // groups
    slots, val, _ = occ.shape
    other_t = lax.rem(t + 1, ntr)
    own_cols = pl.ds(pl.multiple_of(t * cond, cond), cond)
    other_cols = pl.ds(pl.multiple_of(other_t * cond, cond), cond)

    occ_copy = pltpu.make_async_copy(occ_hbm, occ, load_sem.at[0])
    pair_copy = pltpu.make_async_copy(pair_hbm, pair, load_sem.at[1])
    occ_copy.start()
    pair_copy.start()

    virt_copy = pltpu.make_async_copy(virt_hbm, virt, load_sem.at[2])
    virt_copy.start()

    everyone = [(da, dt) for da in range(naux) for dt in range(ntr) if (da, dt) != (0, 0)]

    def peer(da, dt):
        return {"aux": lax.rem(a + da, naux), "tr": lax.rem(t + dt, ntr)}

    barrier = pltpu.get_barrier_semaphore()
    for da, dt in everyone:
        pl.semaphore_signal(barrier, inc=1, device_id=peer(da, dt), device_id_type=MESH)
    pl.semaphore_signal(barrier, inc=1, device_id={"grp": 1 - g}, device_id_type=MESH)

    square = (own_val, own_val)
    diagonal = lax.broadcasted_iota(jnp.int32, square, 0) == lax.broadcasted_iota(jnp.int32, square, 1)
    val_column = jnp.sum(jnp.where(diagonal, val_ref[...], 0.0), axis=1, keepdims=True)
    gap = cond_ref[...] - val_column
    for k in range(vectors):
        trial_k[k] = trial_ref[:, k, :]

    def to_all(it, send, recv, ssem, rsem):
        copies = []
        for da, dt in everyone:
            n = da * ntr + dt
            copies.append(pltpu.make_async_remote_copy(
                src_ref=send.at[it], dst_ref=recv.at[it, n],
                send_sem=ssem.at[it, n], recv_sem=rsem.at[it, n],
                device_id=peer(da, dt), device_id_type=MESH))
        return copies

    def apply(it, x):
        for r in range(groups):
            block = jnp.concatenate(x[r * size:(r + 1) * size], axis=1).astype(BF16)
            block_send[it, r] = block
            block_recv[it, r, a] = block
        if it == 0:
            pl.semaphore_wait(barrier, len(everyone) + 1)
        gathers = []
        for r in range(groups):
            gathers.append([])
            for d in range(1, naux):
                copy = pltpu.make_async_remote_copy(
                    src_ref=block_send.at[it, r], dst_ref=block_recv.at[it, r, a],
                    send_sem=block_ssem.at[it, r, d], recv_sem=block_rsem.at[it, r, d],
                    device_id=peer(d, 0), device_id_type=MESH)
                copy.start()
                gathers[r].append(copy)

        if it == 0:
            pair_copy.wait()
        for k in range(half):
            mixed[:, k, :] = x[k]
        proj = jnp.zeros((half, pair.shape[2]), F32)
        for v in range(own_val):
            proj += jnp.dot(mixed[v].astype(BF16), pair[v], preferred_element_type=F32)
        proj_send[it] = proj
        projections = to_all(it, proj_send, proj_recv, proj_ssem, proj_rsem)
        for copy in projections:
            copy.start()

        if it == 0:
            occ_copy.wait()
            live = live_ref[...]

            @pl.loop(0, slots)
            def _(p):
                keep = (p < live).astype(F32)
                occ[p] = (occ[p].astype(F32) * keep).astype(BF16)

        tr_copies = []
        for r in range(groups):
            for copy in gathers[r]:
                copy.wait_recv()
            for s in range(naux):
                wide[pl.ds(s * own_val, own_val), :] = block_recv[it, r, s].astype(F32)
            rows = occ[...].reshape(slots * val, val)
            for k in range(size):
                column = wide[:, k * cond:(k + 1) * cond].astype(BF16)
                b = jnp.dot(rows, column, preferred_element_type=F32).astype(BF16)
                for q in range(slots):
                    blended[r, k * val:(k + 1) * val, q * cond:(q + 1) * cond] = b[q * val:(q + 1) * val]
            if it == 0 and r == 0:
                virt_copy.wait()
            tr_send[it, r] = jnp.dot(
                blended[r], virt[:, :, other_cols].reshape(slots * cond, cond),
                preferred_element_type=F32).astype(BF16)
            copy = pltpu.make_async_remote_copy(
                src_ref=tr_send.at[it, r], dst_ref=tr_recv.at[it, r],
                send_sem=tr_ssem.at[it, r], recv_sem=tr_rsem.at[it, r],
                device_id=peer(0, 1), device_id_type=MESH)
            copy.start()
            tr_copies.append(copy)

        sums = []
        for r in range(groups):
            acc[...] = jnp.dot(
                blended[r], virt[:, :, own_cols].reshape(slots * cond, cond),
                preferred_element_type=F32)
            tr_copies[r].wait_recv()
            acc[...] += tr_recv[it, r].astype(F32)
            for s in range(naux):
                for k in range(size):
                    row = k * val + s * own_val
                    sum_send[it, r, s, :, k * cond:(k + 1) * cond] = acc[row:row + own_val, :].astype(BF16)
            for d in range(1, naux):
                copy = pltpu.make_async_remote_copy(
                    src_ref=sum_send.at[it, r, lax.rem(a + d, naux)], dst_ref=sum_recv.at[it, r, d],
                    send_sem=sum_ssem.at[it, r, d], recv_sem=sum_rsem.at[it, r, d],
                    device_id=peer(d, 0), device_id_type=MESH)
                copy.start()
                sums.append(copy)

        for copy in projections:
            copy.wait_recv()
        proj = proj_send[it]
        for da, dt in everyone:
            proj += proj_recv[it, da * ntr + dt]
        proj_b = proj.astype(BF16)
        for v in range(own_val):
            mixed[v] = lax.dot_general(
                proj_b, pair[v], (((1,), (1,)), ((), ())), preferred_element_type=F32)
        for copy in sums:
            copy.wait_recv()
        result = []
        for r in range(groups):
            total = sum_send[it, r, a].astype(F32)
            for d in range(1, naux):
                total += sum_recv[it, r, d].astype(F32)
            for k in range(size):
                n = r * size + k
                result.append(gap * x[n] + total[:, k * cond:(k + 1) * cond] + mixed[:, n, :])
        for copy in [c for part in gathers for c in part] + projections + sums + tr_copies:
            copy.wait_send()
        return result

    first = apply(0, [trial_k[g * half + k] for k in range(half)])

    trial = trial_k[...]
    lanes = lax.broadcasted_iota(jnp.int32, (vectors, 128), 1)
    partial = jnp.zeros((vectors, 128), F32)
    for j in range(half):
        lanewise = jnp.sum(trial * first[j][None], axis=1)
        column = jnp.sum(lanewise, axis=1, keepdims=True)
        partial += jnp.where(lanes == g * half + j, column, 0.0)
    dots_send[0] = partial
    dots = to_all(0, dots_send, dots_recv, dots_ssem, dots_rsem)
    for copy in dots:
        copy.start()
    for copy in dots:
        copy.wait()
    for da, dt in everyone:
        partial += dots_recv[0, da * ntr + dt]
    inter = partial / (naux * own_val * ntr * cond)
    dots_send[1] = inter
    core_dots = pltpu.make_async_remote_copy(
        src_ref=dots_send.at[1], dst_ref=core_recv,
        send_sem=core_ssem.at[0], recv_sem=core_rsem.at[0],
        device_id={"grp": 1 - g}, device_id_type=MESH)
    core_dots.start()

    correction = []
    for j in range(half):
        column = jnp.sum(jnp.where(lanes == g * half + j, inter, 0.0), axis=1, keepdims=True)
        fitted = trial_k[0] * column[0:1, :]
        for k in range(1, vectors):
            fitted += trial_k[k] * column[k:k + 1, :]
        correction.append((first[j] - fitted) / gap)

    second = apply(1, correction)
    for k in range(half):
        final_send[k] = second[k]
        out_ref[g * half + k] = second[k]
    final_copy = pltpu.make_async_remote_copy(
        src_ref=final_send, dst_ref=final_recv,
        send_sem=core_ssem.at[1], recv_sem=core_rsem.at[1],
        device_id={"grp": 1 - g}, device_id_type=MESH)
    final_copy.start()
    core_dots.wait()
    inter_ref[...] = (dots_send[1] + core_recv[...])[:, :vectors]
    final_copy.wait()
    for k in range(half):
        out_ref[(1 - g) * half + k] = final_recv[k]


def finish(applied_ref, inter_ref, out_ref, inter_out_ref):
    for k in range(applied_ref.shape[0]):
        out_ref[:, k, :] = applied_ref[k]
    inter_out_ref[...] = inter_ref[...]


def body(naux, ntr, trial_vectors, energy_val, energy_cond, coef_occ, coef_virt, pair_coef, live_aux):
    own_val, vectors, cond = trial_vectors.shape
    slots, val, _ = coef_occ.shape
    naux_all = pair_coef.shape[2]
    half = vectors // 2
    groups = GROUPS
    size = half // groups
    peers = naux * ntr
    vmem = pl.BlockSpec(memory_space=pltpu.VMEM)
    hbm = pl.BlockSpec(memory_space=pl.ANY)
    dma = pltpu.SemaphoreType.DMA
    scratch = [
        pltpu.VMEM(coef_occ.shape, BF16),
        pltpu.VMEM(coef_virt.shape, BF16),
        pltpu.VMEM(pair_coef.shape, BF16),
        pltpu.VMEM((groups, size * val, slots * cond), BF16),
        pltpu.VMEM((size * val, cond), F32),
        pltpu.VMEM((val, size * cond), F32),
        pltpu.VMEM((own_val, half, cond), F32),
        pltpu.VMEM((vectors, own_val, cond), F32),
        pltpu.VMEM((2, groups, own_val, size * cond), BF16),
        pltpu.VMEM((2, groups, naux, own_val, size * cond), BF16),
        pltpu.VMEM((2, half, naux_all), F32),
        pltpu.VMEM((2, peers, half, naux_all), F32),
        pltpu.VMEM((2, groups, size * val, cond), BF16),
        pltpu.VMEM((2, groups, size * val, cond), BF16),
        pltpu.VMEM((2, groups, naux, own_val, size * cond), BF16),
        pltpu.VMEM((2, groups, naux, own_val, size * cond), BF16),
        pltpu.VMEM((2, vectors, 128), F32),
        pltpu.VMEM((1, peers, vectors, 128), F32),
        pltpu.VMEM((vectors, 128), F32),
        pltpu.VMEM((half, own_val, cond), F32),
        pltpu.VMEM((half, own_val, cond), F32),
        dma((3,)),
        dma((2, groups, naux)), dma((2, groups, naux)),
        dma((2, peers)), dma((2, peers)),
        dma((2, groups)), dma((2, groups)),
        dma((2, groups, naux)), dma((2, groups, naux)),
        dma((1, peers)), dma((1, peers)),
        dma((2,)), dma((2,)),
    ]
    applied, intersection = pl.pallas_call(
        functools.partial(kernel, naux, ntr, groups),
        out_shape=(
            jax.ShapeDtypeStruct((vectors, own_val, cond), F32),
            jax.ShapeDtypeStruct((vectors, vectors), F32),
        ),
        in_specs=[vmem, vmem, vmem, vmem, hbm, hbm, hbm],
        out_specs=(vmem, vmem),
        scratch_shapes=scratch,
        compiler_params=pltpu.CompilerParams(
            collective_id=0, has_side_effects=True, vmem_limit_bytes=56 * 1024 * 1024
        ),
    )(
        live_aux.reshape(1, 1), trial_vectors, energy_val.reshape(1, -1),
        energy_cond.reshape(1, -1), coef_occ, coef_virt, pair_coef,
    )
    return pl.pallas_call(
        finish,
        out_shape=(
            jax.ShapeDtypeStruct(trial_vectors.shape, F32),
            jax.ShapeDtypeStruct((vectors, vectors), F32),
        ),
        in_specs=[vmem, vmem],
        out_specs=(vmem, vmem),
    )(applied, intersection)


def solution(mesh):
    in_specs = (
        P("aux", None, "tr"),
        P("aux"),
        P("tr"),
        P("aux", None, None),
        P("aux", "tr", None),
        P("aux", "tr", None),
        P("aux"),
    )
    out_specs = (P("aux", None, "tr"), P())
    sizes = (mesh.shape["aux"], mesh.shape["tr"])
    return jax.shard_map(
        functools.partial(body, *sizes), mesh=mesh, in_specs=in_specs, out_specs=out_specs, check_vma=False
    )
```

```python
import functools

import jax
import jax.numpy as jnp
from jax import lax
from jax.experimental import pallas as pl
from jax.experimental.pallas import tpu as pltpu
from jax.sharding import PartitionSpec as P

F32 = jnp.float32
BF16 = jnp.bfloat16
GROUPS = 1
CHUNK = 16
BLEND = 16
MESH = pl.DeviceIdType.MESH


def kernel(
    naux, ntr, groups,
    live_ref, trial_ref, val_ref, cond_ref, occ_hbm, virt_hbm, pair_hbm,
    out_ref, inter_ref,
    occ, virt, pair, blended, acc, wide, mixed, trial_k,
    block_send, block_recv, proj_send, proj_recv, tr_send, tr_recv,
    sum_send, sum_recv, dots_send, dots_recv, core_recv, final_send, final_recv,
    load_sem, block_ssem, block_rsem, proj_ssem, proj_rsem,
    tr_ssem, tr_rsem, sum_ssem, sum_rsem, dots_ssem, dots_rsem, core_ssem, core_rsem,
):
    g = lax.axis_index("grp")
    a = lax.axis_index("aux")
    t = lax.axis_index("tr")
    own_val, vectors, cond = trial_ref.shape
    half = vectors // 2
    size = half // groups
    slots, val, _ = occ.shape
    other_t = lax.rem(t + 1, ntr)
    own_cols = pl.ds(pl.multiple_of(t * cond, cond), cond)
    other_cols = pl.ds(pl.multiple_of(other_t * cond, cond), cond)

    occ_copy = pltpu.make_async_copy(occ_hbm, occ, load_sem.at[0])
    pair_copy = pltpu.make_async_copy(pair_hbm, pair, load_sem.at[1])
    occ_copy.start()
    pair_copy.start()

    virt_copy = pltpu.make_async_copy(virt_hbm, virt, load_sem.at[2])
    virt_copy.start()

    everyone = [(da, dt) for da in range(naux) for dt in range(ntr) if (da, dt) != (0, 0)]

    def peer(da, dt):
        return {"aux": lax.rem(a + da, naux), "tr": lax.rem(t + dt, ntr)}

    barrier = pltpu.get_barrier_semaphore()
    for da, dt in everyone:
        pl.semaphore_signal(barrier, inc=1, device_id=peer(da, dt), device_id_type=MESH)
    pl.semaphore_signal(barrier, inc=1, device_id={"grp": 1 - g}, device_id_type=MESH)

    square = (own_val, own_val)
    diagonal = lax.broadcasted_iota(jnp.int32, square, 0) == lax.broadcasted_iota(jnp.int32, square, 1)
    val_column = jnp.sum(jnp.where(diagonal, val_ref[...], 0.0), axis=1, keepdims=True)
    gap = cond_ref[...] - val_column
    for k in range(vectors):
        trial_k[k] = trial_ref[:, k, :]

    def to_all(it, send, recv, ssem, rsem):
        copies = []
        for da, dt in everyone:
            n = da * ntr + dt
            copies.append(pltpu.make_async_remote_copy(
                src_ref=send.at[it], dst_ref=recv.at[it, n],
                send_sem=ssem.at[it, n], recv_sem=rsem.at[it, n],
                device_id=peer(da, dt), device_id_type=MESH))
        return copies

    def contract(r, cols):
        acc[...] = jnp.zeros_like(acc)

        @pl.loop(0, slots // CHUNK)
        def _(i):
            acc[...] += jnp.dot(
                blended[r, i], virt[pl.ds(i * CHUNK, CHUNK), :, cols].reshape(CHUNK * cond, cond),
                preferred_element_type=F32)

    def apply(it, x):
        for r in range(groups):
            block = jnp.concatenate(x[r * size:(r + 1) * size], axis=1).astype(BF16)
            block_send[it, r] = block
            block_recv[it, r, a] = block
        if it == 0:
            pl.semaphore_wait(barrier, len(everyone) + 1)
        gathers = []
        for r in range(groups):
            gathers.append([])
            for d in range(1, naux):
                copy = pltpu.make_async_remote_copy(
                    src_ref=block_send.at[it, r], dst_ref=block_recv.at[it, r, a],
                    send_sem=block_ssem.at[it, r, d], recv_sem=block_rsem.at[it, r, d],
                    device_id=peer(d, 0), device_id_type=MESH)
                copy.start()
                gathers[r].append(copy)

        if it == 0:
            pair_copy.wait()
        for k in range(half):
            mixed[:, k, :] = x[k]
        proj = jnp.zeros((half, pair.shape[2]), F32)
        for v in range(own_val):
            proj += jnp.dot(mixed[v].astype(BF16), pair[v], preferred_element_type=F32)
        proj_send[it] = proj
        projections = to_all(it, proj_send, proj_recv, proj_ssem, proj_rsem)
        for copy in projections:
            copy.start()

        if it == 0:
            occ_copy.wait()
            live = live_ref[...]

            @pl.loop(0, slots)
            def _(p):
                keep = (p < live).astype(F32)
                occ[p] = (occ[p].astype(F32) * keep).astype(BF16)

        tr_copies = []
        for r in range(groups):
            for copy in gathers[r]:
                copy.wait_recv()
            for s in range(naux):
                wide[pl.ds(s * own_val, own_val), :] = block_recv[it, r, s].astype(F32)
            columns = [wide[:, k * cond:(k + 1) * cond].astype(BF16) for k in range(size)]

            @pl.loop(0, slots // BLEND)
            def _(i):
                rows = occ[pl.ds(i * BLEND, BLEND)].reshape(BLEND * val, val)
                for k in range(size):
                    b = jnp.dot(rows, columns[k], preferred_element_type=F32).astype(BF16)
                    for q in range(BLEND):
                        blended[r, i * (BLEND // CHUNK) + q // CHUNK, k * val:(k + 1) * val,
                                (q % CHUNK) * cond:(q % CHUNK + 1) * cond] = b[q * val:(q + 1) * val]

            if it == 0 and r == 0:
                virt_copy.wait()
            contract(r, other_cols)
            tr_send[it, r] = acc[...].astype(BF16)
            copy = pltpu.make_async_remote_copy(
                src_ref=tr_send.at[it, r], dst_ref=tr_recv.at[it, r],
                send_sem=tr_ssem.at[it, r], recv_sem=tr_rsem.at[it, r],
                device_id=peer(0, 1), device_id_type=MESH)
            copy.start()
            tr_copies.append(copy)

        sums = []
        for r in range(groups):
            contract(r, own_cols)
            tr_copies[r].wait_recv()
            acc[...] += tr_recv[it, r].astype(F32)
            for s in range(naux):
                for k in range(size):
                    row = k * val + s * own_val
                    sum_send[it, r, s, :, k * cond:(k + 1) * cond] = acc[row:row + own_val, :].astype(BF16)
            for d in range(1, naux):
                copy = pltpu.make_async_remote_copy(
                    src_ref=sum_send.at[it, r, lax.rem(a + d, naux)], dst_ref=sum_recv.at[it, r, d],
                    send_sem=sum_ssem.at[it, r, d], recv_sem=sum_rsem.at[it, r, d],
                    device_id=peer(d, 0), device_id_type=MESH)
                copy.start()
                sums.append(copy)

        for copy in projections:
            copy.wait_recv()
        proj = proj_send[it]
        for da, dt in everyone:
            proj += proj_recv[it, da * ntr + dt]
        proj_b = proj.astype(BF16)
        for v in range(own_val):
            mixed[v] = lax.dot_general(
                proj_b, pair[v], (((1,), (1,)), ((), ())), preferred_element_type=F32)
        for copy in sums:
            copy.wait_recv()
        result = []
        for r in range(groups):
            total = sum_send[it, r, a].astype(F32)
            for d in range(1, naux):
                total += sum_recv[it, r, d].astype(F32)
            for k in range(size):
                n = r * size + k
                result.append(gap * x[n] + total[:, k * cond:(k + 1) * cond] + mixed[:, n, :])
        for copy in [c for part in gathers for c in part] + projections + sums + tr_copies:
            copy.wait_send()
        return result

    first = apply(0, [trial_k[g * half + k] for k in range(half)])

    trial = trial_k[...]
    lanes = lax.broadcasted_iota(jnp.int32, (vectors, 128), 1)
    partial = jnp.zeros((vectors, 128), F32)
    for j in range(half):
        lanewise = jnp.sum(trial * first[j][None], axis=1)
        column = jnp.sum(lanewise, axis=1, keepdims=True)
        partial += jnp.where(lanes == g * half + j, column, 0.0)
    dots_send[0] = partial
    dots = to_all(0, dots_send, dots_recv, dots_ssem, dots_rsem)
    for copy in dots:
        copy.start()
    for copy in dots:
        copy.wait()
    for da, dt in everyone:
        partial += dots_recv[0, da * ntr + dt]
    inter = partial / (naux * own_val * ntr * cond)
    dots_send[1] = inter
    core_dots = pltpu.make_async_remote_copy(
        src_ref=dots_send.at[1], dst_ref=core_recv,
        send_sem=core_ssem.at[0], recv_sem=core_rsem.at[0],
        device_id={"grp": 1 - g}, device_id_type=MESH)
    core_dots.start()

    correction = []
    for j in range(half):
        column = jnp.sum(jnp.where(lanes == g * half + j, inter, 0.0), axis=1, keepdims=True)
        fitted = trial_k[0] * column[0:1, :]
        for k in range(1, vectors):
            fitted += trial_k[k] * column[k:k + 1, :]
        correction.append((first[j] - fitted) / gap)

    second = apply(1, correction)
    for k in range(half):
        final_send[k] = second[k]
        out_ref[g * half + k] = second[k]
    final_copy = pltpu.make_async_remote_copy(
        src_ref=final_send, dst_ref=final_recv,
        send_sem=core_ssem.at[1], recv_sem=core_rsem.at[1],
        device_id={"grp": 1 - g}, device_id_type=MESH)
    final_copy.start()
    core_dots.wait()
    inter_ref[...] = (dots_send[1] + core_recv[...])[:, :vectors]
    final_copy.wait()
    for k in range(half):
        out_ref[(1 - g) * half + k] = final_recv[k]


def finish(applied_ref, inter_ref, out_ref, inter_out_ref):
    for k in range(applied_ref.shape[0]):
        out_ref[:, k, :] = applied_ref[k]
    inter_out_ref[...] = inter_ref[...]


def body(naux, ntr, trial_vectors, energy_val, energy_cond, coef_occ, coef_virt, pair_coef, live_aux):
    own_val, vectors, cond = trial_vectors.shape
    slots, val, _ = coef_occ.shape
    naux_all = pair_coef.shape[2]
    half = vectors // 2
    groups = GROUPS
    size = half // groups
    peers = naux * ntr
    vmem = pl.BlockSpec(memory_space=pltpu.VMEM)
    hbm = pl.BlockSpec(memory_space=pl.ANY)
    dma = pltpu.SemaphoreType.DMA
    scratch = [
        pltpu.VMEM(coef_occ.shape, BF16),
        pltpu.VMEM(coef_virt.shape, BF16),
        pltpu.VMEM(pair_coef.shape, BF16),
        pltpu.VMEM((groups, slots // CHUNK, size * val, CHUNK * cond), BF16),
        pltpu.VMEM((size * val, cond), F32),
        pltpu.VMEM((val, size * cond), F32),
        pltpu.VMEM((own_val, half, cond), F32),
        pltpu.VMEM((vectors, own_val, cond), F32),
        pltpu.VMEM((2, groups, own_val, size * cond), BF16),
        pltpu.VMEM((2, groups, naux, own_val, size * cond), BF16),
        pltpu.VMEM((2, half, naux_all), F32),
        pltpu.VMEM((2, peers, half, naux_all), F32),
        pltpu.VMEM((2, groups, size * val, cond), BF16),
        pltpu.VMEM((2, groups, size * val, cond), BF16),
        pltpu.VMEM((2, groups, naux, own_val, size * cond), BF16),
        pltpu.VMEM((2, groups, naux, own_val, size * cond), BF16),
        pltpu.VMEM((2, vectors, 128), F32),
        pltpu.VMEM((1, peers, vectors, 128), F32),
        pltpu.VMEM((vectors, 128), F32),
        pltpu.VMEM((half, own_val, cond), F32),
        pltpu.VMEM((half, own_val, cond), F32),
        dma((3,)),
        dma((2, groups, naux)), dma((2, groups, naux)),
        dma((2, peers)), dma((2, peers)),
        dma((2, groups)), dma((2, groups)),
        dma((2, groups, naux)), dma((2, groups, naux)),
        dma((1, peers)), dma((1, peers)),
        dma((2,)), dma((2,)),
    ]
    applied, intersection = pl.pallas_call(
        functools.partial(kernel, naux, ntr, groups),
        out_shape=(
            jax.ShapeDtypeStruct((vectors, own_val, cond), F32),
            jax.ShapeDtypeStruct((vectors, vectors), F32),
        ),
        in_specs=[vmem, vmem, vmem, vmem, hbm, hbm, hbm],
        out_specs=(vmem, vmem),
        scratch_shapes=scratch,
        compiler_params=pltpu.CompilerParams(
            collective_id=0, has_side_effects=True, vmem_limit_bytes=56 * 1024 * 1024
        ),
    )(
        live_aux.reshape(1, 1), trial_vectors, energy_val.reshape(1, -1),
        energy_cond.reshape(1, -1), coef_occ, coef_virt, pair_coef,
    )
    return pl.pallas_call(
        finish,
        out_shape=(
            jax.ShapeDtypeStruct(trial_vectors.shape, F32),
            jax.ShapeDtypeStruct((vectors, vectors), F32),
        ),
        in_specs=[vmem, vmem],
        out_specs=(vmem, vmem),
    )(applied, intersection)


def solution(mesh):
    in_specs = (
        P("aux", None, "tr"),
        P("aux"),
        P("tr"),
        P("aux", None, None),
        P("aux", "tr", None),
        P("aux", "tr", None),
        P("aux"),
    )
    out_specs = (P("aux", None, "tr"), P())
    sizes = (mesh.shape["aux"], mesh.shape["tr"])
    return jax.shard_map(
        functools.partial(body, *sizes), mesh=mesh, in_specs=in_specs, out_specs=out_specs, check_vma=False
    )
```

```python
import functools

import jax
import jax.numpy as jnp
from jax import lax
from jax.experimental import pallas as pl
from jax.experimental.pallas import tpu as pltpu
from jax.sharding import PartitionSpec as P

F32 = jnp.float32
BF16 = jnp.bfloat16
GROUPS = 1
CHUNK = 16
BLEND = 32
MESH = pl.DeviceIdType.MESH


def kernel(
    naux, ntr, groups,
    live_ref, trial_ref, val_ref, cond_ref, occ_hbm, virt_hbm, pair_hbm,
    out_ref, inter_ref,
    occ, virt, pair, blended, acc, wide, mixed, trial_k,
    block_send, block_recv, proj_send, proj_recv, tr_send, tr_recv,
    sum_send, sum_recv, dots_send, dots_recv, core_recv, final_send, final_recv,
    load_sem, block_ssem, block_rsem, proj_ssem, proj_rsem,
    tr_ssem, tr_rsem, sum_ssem, sum_rsem, dots_ssem, dots_rsem, core_ssem, core_rsem,
):
    g = lax.axis_index("grp")
    a = lax.axis_index("aux")
    t = lax.axis_index("tr")
    own_val, vectors, cond = trial_ref.shape
    half = vectors // 2
    size = half // groups
    slots, val, _ = occ.shape
    other_t = lax.rem(t + 1, ntr)
    own_cols = pl.ds(pl.multiple_of(t * cond, cond), cond)
    other_cols = pl.ds(pl.multiple_of(other_t * cond, cond), cond)

    occ_copy = pltpu.make_async_copy(occ_hbm, occ, load_sem.at[0])
    pair_copy = pltpu.make_async_copy(pair_hbm, pair, load_sem.at[1])
    occ_copy.start()
    pair_copy.start()

    virt_copy = pltpu.make_async_copy(virt_hbm, virt, load_sem.at[2])
    virt_copy.start()

    everyone = [(da, dt) for da in range(naux) for dt in range(ntr) if (da, dt) != (0, 0)]

    def peer(da, dt):
        return {"aux": lax.rem(a + da, naux), "tr": lax.rem(t + dt, ntr)}

    barrier = pltpu.get_barrier_semaphore()
    for da, dt in everyone:
        pl.semaphore_signal(barrier, inc=1, device_id=peer(da, dt), device_id_type=MESH)
    pl.semaphore_signal(barrier, inc=1, device_id={"grp": 1 - g}, device_id_type=MESH)

    square = (own_val, own_val)
    diagonal = lax.broadcasted_iota(jnp.int32, square, 0) == lax.broadcasted_iota(jnp.int32, square, 1)
    val_column = jnp.sum(jnp.where(diagonal, val_ref[...], 0.0), axis=1, keepdims=True)
    gap = cond_ref[...] - val_column
    for k in range(vectors):
        trial_k[k] = trial_ref[:, k, :]

    def to_all(it, send, recv, ssem, rsem):
        copies = []
        for da, dt in everyone:
            n = da * ntr + dt
            copies.append(pltpu.make_async_remote_copy(
                src_ref=send.at[it], dst_ref=recv.at[it, n],
                send_sem=ssem.at[it, n], recv_sem=rsem.at[it, n],
                device_id=peer(da, dt), device_id_type=MESH))
        return copies

    def contract(r, cols):
        acc[...] = jnp.zeros_like(acc)

        @pl.loop(0, slots // CHUNK)
        def _(i):
            acc[...] += jnp.dot(
                blended[r, i], virt[pl.ds(i * CHUNK, CHUNK), :, cols].reshape(CHUNK * cond, cond),
                preferred_element_type=F32)

    def apply(it, x):
        for r in range(groups):
            block = jnp.concatenate(x[r * size:(r + 1) * size], axis=1).astype(BF16)
            block_send[it, r] = block
            block_recv[it, r, a] = block
        if it == 0:
            pl.semaphore_wait(barrier, len(everyone) + 1)
        gathers = []
        for r in range(groups):
            gathers.append([])
            for d in range(1, naux):
                copy = pltpu.make_async_remote_copy(
                    src_ref=block_send.at[it, r], dst_ref=block_recv.at[it, r, a],
                    send_sem=block_ssem.at[it, r, d], recv_sem=block_rsem.at[it, r, d],
                    device_id=peer(d, 0), device_id_type=MESH)
                copy.start()
                gathers[r].append(copy)

        if it == 0:
            pair_copy.wait()
        for k in range(half):
            mixed[:, k, :] = x[k]
        proj = jnp.zeros((half, pair.shape[2]), F32)
        for v in range(own_val):
            proj += jnp.dot(mixed[v].astype(BF16), pair[v], preferred_element_type=F32)
        proj_send[it] = proj.astype(BF16)
        projections = to_all(it, proj_send, proj_recv, proj_ssem, proj_rsem)
        for copy in projections:
            copy.start()

        if it == 0:
            occ_copy.wait()
            live = live_ref[...]

            @pl.loop(0, slots)
            def _(p):
                keep = (p < live).astype(F32)
                occ[p] = (occ[p].astype(F32) * keep).astype(BF16)

        tr_copies = []
        for r in range(groups):
            for copy in gathers[r]:
                copy.wait_recv()
            for s in range(naux):
                wide[pl.ds(s * own_val, own_val), :] = block_recv[it, r, s].astype(F32)
            columns = [wide[:, k * cond:(k + 1) * cond].astype(BF16) for k in range(size)]

            @pl.loop(0, slots // BLEND)
            def _(i):
                rows = occ[pl.ds(i * BLEND, BLEND)].reshape(BLEND * val, val)
                for k in range(size):
                    b = jnp.dot(rows, columns[k], preferred_element_type=F32).astype(BF16)
                    for q in range(BLEND):
                        blended[r, i * (BLEND // CHUNK) + q // CHUNK, k * val:(k + 1) * val,
                                (q % CHUNK) * cond:(q % CHUNK + 1) * cond] = b[q * val:(q + 1) * val]

            if it == 0 and r == 0:
                virt_copy.wait()
            copy = pltpu.make_async_remote_copy(
                src_ref=tr_send.at[it, r], dst_ref=tr_recv.at[it, r],
                send_sem=tr_ssem.at[it, r], recv_sem=tr_rsem.at[it, r],
                device_id=peer(0, 1), device_id_type=MESH)
            tr_copies.append(copy)

            @pl.loop(0, 2)
            def _(j):
                start = pl.multiple_of(lax.rem(t + 1 + j, ntr) * cond, cond)
                contract(r, pl.ds(start, cond))

                @pl.when(j == 0)
                def _():
                    tr_send[it, r] = acc[...].astype(BF16)
                    copy.start()

        sums = []
        for r in range(groups):
            tr_copies[r].wait_recv()
            acc[...] += tr_recv[it, r].astype(F32)
            for s in range(naux):
                for k in range(size):
                    row = k * val + s * own_val
                    sum_send[it, r, s, :, k * cond:(k + 1) * cond] = acc[row:row + own_val, :].astype(BF16)
            for d in range(1, naux):
                copy = pltpu.make_async_remote_copy(
                    src_ref=sum_send.at[it, r, lax.rem(a + d, naux)], dst_ref=sum_recv.at[it, r, d],
                    send_sem=sum_ssem.at[it, r, d], recv_sem=sum_rsem.at[it, r, d],
                    device_id=peer(d, 0), device_id_type=MESH)
                copy.start()
                sums.append(copy)

        for copy in projections:
            copy.wait_recv()
        proj = proj_send[it].astype(F32)
        for da, dt in everyone:
            proj += proj_recv[it, da * ntr + dt].astype(F32)
        proj_b = proj.astype(BF16)
        for v in range(own_val):
            mixed[v] = lax.dot_general(
                proj_b, pair[v], (((1,), (1,)), ((), ())), preferred_element_type=F32)
        for copy in sums:
            copy.wait_recv()
        result = []
        for r in range(groups):
            total = sum_send[it, r, a].astype(F32)
            for d in range(1, naux):
                total += sum_recv[it, r, d].astype(F32)
            for k in range(size):
                n = r * size + k
                result.append(gap * x[n] + total[:, k * cond:(k + 1) * cond] + mixed[:, n, :])
        for copy in [c for part in gathers for c in part] + projections + sums + tr_copies:
            copy.wait_send()
        return result

    first = apply(0, [trial_k[g * half + k] for k in range(half)])

    trial = trial_k[...]
    lanes = lax.broadcasted_iota(jnp.int32, (vectors, 128), 1)
    partial = jnp.zeros((vectors, 128), F32)
    for j in range(half):
        lanewise = jnp.sum(trial * first[j][None], axis=1)
        column = jnp.sum(lanewise, axis=1, keepdims=True)
        partial += jnp.where(lanes == g * half + j, column, 0.0)
    dots_send[0] = partial
    dots = to_all(0, dots_send, dots_recv, dots_ssem, dots_rsem)
    for copy in dots:
        copy.start()
    for copy in dots:
        copy.wait()
    for da, dt in everyone:
        partial += dots_recv[0, da * ntr + dt]
    inter = partial / (naux * own_val * ntr * cond)
    dots_send[1] = inter
    core_dots = pltpu.make_async_remote_copy(
        src_ref=dots_send.at[1], dst_ref=core_recv,
        send_sem=core_ssem.at[0], recv_sem=core_rsem.at[0],
        device_id={"grp": 1 - g}, device_id_type=MESH)
    core_dots.start()

    correction = []
    for j in range(half):
        column = jnp.sum(jnp.where(lanes == g * half + j, inter, 0.0), axis=1, keepdims=True)
        fitted = trial_k[0] * column[0:1, :]
        for k in range(1, vectors):
            fitted += trial_k[k] * column[k:k + 1, :]
        correction.append((first[j] - fitted) / gap)

    second = apply(1, correction)
    for k in range(half):
        final_send[k] = second[k]
        out_ref[g * half + k] = second[k]
    final_copy = pltpu.make_async_remote_copy(
        src_ref=final_send, dst_ref=final_recv,
        send_sem=core_ssem.at[1], recv_sem=core_rsem.at[1],
        device_id={"grp": 1 - g}, device_id_type=MESH)
    final_copy.start()
    core_dots.wait()
    inter_ref[...] = (dots_send[1] + core_recv[...])[:, :vectors]
    final_copy.wait()
    for k in range(half):
        out_ref[(1 - g) * half + k] = final_recv[k]


def finish(applied_ref, inter_ref, out_ref, inter_out_ref):
    for k in range(applied_ref.shape[0]):
        out_ref[:, k, :] = applied_ref[k]
    inter_out_ref[...] = inter_ref[...]


def body(naux, ntr, trial_vectors, energy_val, energy_cond, coef_occ, coef_virt, pair_coef, live_aux):
    own_val, vectors, cond = trial_vectors.shape
    slots, val, _ = coef_occ.shape
    naux_all = pair_coef.shape[2]
    half = vectors // 2
    groups = GROUPS
    size = half // groups
    peers = naux * ntr
    vmem = pl.BlockSpec(memory_space=pltpu.VMEM)
    hbm = pl.BlockSpec(memory_space=pl.ANY)
    dma = pltpu.SemaphoreType.DMA
    scratch = [
        pltpu.VMEM(coef_occ.shape, BF16),
        pltpu.VMEM(coef_virt.shape, BF16),
        pltpu.VMEM(pair_coef.shape, BF16),
        pltpu.VMEM((groups, slots // CHUNK, size * val, CHUNK * cond), BF16),
        pltpu.VMEM((size * val, cond), F32),
        pltpu.VMEM((val, size * cond), F32),
        pltpu.VMEM((own_val, half, cond), F32),
        pltpu.VMEM((vectors, own_val, cond), F32),
        pltpu.VMEM((2, groups, own_val, size * cond), BF16),
        pltpu.VMEM((2, groups, naux, own_val, size * cond), BF16),
        pltpu.VMEM((2, half, naux_all), BF16),
        pltpu.VMEM((2, peers, half, naux_all), BF16),
        pltpu.VMEM((2, groups, size * val, cond), BF16),
        pltpu.VMEM((2, groups, size * val, cond), BF16),
        pltpu.VMEM((2, groups, naux, own_val, size * cond), BF16),
        pltpu.VMEM((2, groups, naux, own_val, size * cond), BF16),
        pltpu.VMEM((2, vectors, 128), F32),
        pltpu.VMEM((1, peers, vectors, 128), F32),
        pltpu.VMEM((vectors, 128), F32),
        pltpu.VMEM((half, own_val, cond), F32),
        pltpu.VMEM((half, own_val, cond), F32),
        dma((3,)),
        dma((2, groups, naux)), dma((2, groups, naux)),
        dma((2, peers)), dma((2, peers)),
        dma((2, groups)), dma((2, groups)),
        dma((2, groups, naux)), dma((2, groups, naux)),
        dma((1, peers)), dma((1, peers)),
        dma((2,)), dma((2,)),
    ]
    applied, intersection = pl.pallas_call(
        functools.partial(kernel, naux, ntr, groups),
        out_shape=(
            jax.ShapeDtypeStruct((vectors, own_val, cond), F32),
            jax.ShapeDtypeStruct((vectors, vectors), F32),
        ),
        in_specs=[vmem, vmem, vmem, vmem, hbm, hbm, hbm],
        out_specs=(vmem, vmem),
        scratch_shapes=scratch,
        compiler_params=pltpu.CompilerParams(
            collective_id=0, has_side_effects=True, vmem_limit_bytes=56 * 1024 * 1024
        ),
    )(
        live_aux.reshape(1, 1), trial_vectors, energy_val.reshape(1, -1),
        energy_cond.reshape(1, -1), coef_occ, coef_virt, pair_coef,
    )
    return pl.pallas_call(
        finish,
        out_shape=(
            jax.ShapeDtypeStruct(trial_vectors.shape, F32),
            jax.ShapeDtypeStruct((vectors, vectors), F32),
        ),
        in_specs=[vmem, vmem],
        out_specs=(vmem, vmem),
    )(applied, intersection)


def solution(mesh):
    in_specs = (
        P("aux", None, "tr"),
        P("aux"),
        P("tr"),
        P("aux", None, None),
        P("aux", "tr", None),
        P("aux", "tr", None),
        P("aux"),
    )
    out_specs = (P("aux", None, "tr"), P())
    sizes = (mesh.shape["aux"], mesh.shape["tr"])
    return jax.shard_map(
        functools.partial(body, *sizes), mesh=mesh, in_specs=in_specs, out_specs=out_specs, check_vma=False
    )
```

```python
import functools

import jax
import jax.numpy as jnp
from jax import lax
from jax.experimental import pallas as pl
from jax.experimental.pallas import tpu as pltpu
from jax.sharding import PartitionSpec as P

F32 = jnp.float32
BF16 = jnp.bfloat16
GROUPS = 1
CHUNK = 32
BLEND = 32
MESH = pl.DeviceIdType.MESH


def kernel(
    naux, ntr, groups,
    live_ref, trial_ref, val_ref, cond_ref, occ_hbm, virt_hbm, pair_hbm,
    out_ref, inter_ref,
    occ, virt, pair, blended, acc, wide, mixed, trial_k,
    block_send, block_recv, proj_send, proj_recv, tr_send, tr_recv,
    sum_send, sum_recv, dots_send, dots_recv, core_recv, final_send, final_recv,
    load_sem, block_ssem, block_rsem, proj_ssem, proj_rsem,
    tr_ssem, tr_rsem, sum_ssem, sum_rsem, dots_ssem, dots_rsem, core_ssem, core_rsem,
):
    g = lax.axis_index("grp")
    a = lax.axis_index("aux")
    t = lax.axis_index("tr")
    own_val, vectors, cond = trial_ref.shape
    half = vectors // 2
    size = half // groups
    slots, val, _ = occ.shape
    other_t = lax.rem(t + 1, ntr)
    own_cols = pl.ds(pl.multiple_of(t * cond, cond), cond)
    other_cols = pl.ds(pl.multiple_of(other_t * cond, cond), cond)

    occ_copy = pltpu.make_async_copy(occ_hbm, occ, load_sem.at[0])
    pair_copy = pltpu.make_async_copy(pair_hbm, pair, load_sem.at[1])
    occ_copy.start()
    pair_copy.start()

    virt_copy = pltpu.make_async_copy(virt_hbm, virt, load_sem.at[2])
    virt_copy.start()

    everyone = [(da, dt) for da in range(naux) for dt in range(ntr) if (da, dt) != (0, 0)]

    def peer(da, dt):
        return {"aux": lax.rem(a + da, naux), "tr": lax.rem(t + dt, ntr)}

    barrier = pltpu.get_barrier_semaphore()
    for da, dt in everyone:
        pl.semaphore_signal(barrier, inc=1, device_id=peer(da, dt), device_id_type=MESH)
    pl.semaphore_signal(barrier, inc=1, device_id={"grp": 1 - g}, device_id_type=MESH)

    square = (own_val, own_val)
    diagonal = lax.broadcasted_iota(jnp.int32, square, 0) == lax.broadcasted_iota(jnp.int32, square, 1)
    val_column = jnp.sum(jnp.where(diagonal, val_ref[...], 0.0), axis=1, keepdims=True)
    gap = cond_ref[...] - val_column
    for k in range(vectors):
        trial_k[k] = trial_ref[:, k, :]

    def to_all(it, send, recv, ssem, rsem):
        copies = []
        for da, dt in everyone:
            n = da * ntr + dt
            copies.append(pltpu.make_async_remote_copy(
                src_ref=send.at[it], dst_ref=recv.at[it, n],
                send_sem=ssem.at[it, n], recv_sem=rsem.at[it, n],
                device_id=peer(da, dt), device_id_type=MESH))
        return copies

    def contract(r, cols):
        acc[...] = jnp.zeros_like(acc)

        @pl.loop(0, slots // CHUNK)
        def _(i):
            acc[...] += jnp.dot(
                blended[r, i], virt[pl.ds(i * CHUNK, CHUNK), :, cols].reshape(CHUNK * cond, cond),
                preferred_element_type=F32)

    def apply(it, x):
        for r in range(groups):
            block = jnp.concatenate(x[r * size:(r + 1) * size], axis=1).astype(BF16)
            block_send[it, r] = block
            block_recv[it, r, a] = block
        if it == 0:
            pl.semaphore_wait(barrier, len(everyone) + 1)
        gathers = []
        for r in range(groups):
            gathers.append([])
            for d in range(1, naux):
                copy = pltpu.make_async_remote_copy(
                    src_ref=block_send.at[it, r], dst_ref=block_recv.at[it, r, a],
                    send_sem=block_ssem.at[it, r, d], recv_sem=block_rsem.at[it, r, d],
                    device_id=peer(d, 0), device_id_type=MESH)
                copy.start()
                gathers[r].append(copy)

        if it == 0:
            pair_copy.wait()
        for k in range(half):
            mixed[:, k, :] = x[k]
        proj = jnp.zeros((half, pair.shape[2]), F32)
        for v in range(own_val):
            proj += jnp.dot(mixed[v].astype(BF16), pair[v], preferred_element_type=F32)
        proj_send[it] = proj.astype(BF16)
        projections = to_all(it, proj_send, proj_recv, proj_ssem, proj_rsem)
        for copy in projections:
            copy.start()

        if it == 0:
            occ_copy.wait()
            live = live_ref[...]

            @pl.loop(0, slots)
            def _(p):
                keep = (p < live).astype(F32)
                occ[p] = (occ[p].astype(F32) * keep).astype(BF16)

        tr_copies = []
        for r in range(groups):
            for copy in gathers[r]:
                copy.wait_recv()
            for s in range(naux):
                wide[pl.ds(s * own_val, own_val), :] = block_recv[it, r, s].astype(F32)
            columns = [wide[:, k * cond:(k + 1) * cond].astype(BF16) for k in range(size)]

            @pl.loop(0, slots // BLEND)
            def _(i):
                rows = occ[pl.ds(i * BLEND, BLEND)].reshape(BLEND * val, val)
                for k in range(size):
                    b = jnp.dot(rows, columns[k], preferred_element_type=F32).astype(BF16)
                    for q in range(BLEND):
                        blended[r, i * (BLEND // CHUNK) + q // CHUNK, k * val:(k + 1) * val,
                                (q % CHUNK) * cond:(q % CHUNK + 1) * cond] = b[q * val:(q + 1) * val]

            if it == 0 and r == 0:
                virt_copy.wait()
            copy = pltpu.make_async_remote_copy(
                src_ref=tr_send.at[it, r], dst_ref=tr_recv.at[it, r],
                send_sem=tr_ssem.at[it, r], recv_sem=tr_rsem.at[it, r],
                device_id=peer(0, 1), device_id_type=MESH)
            tr_copies.append(copy)

            @pl.loop(0, 2)
            def _(j):
                start = pl.multiple_of(lax.rem(t + 1 + j, ntr) * cond, cond)
                contract(r, pl.ds(start, cond))

                @pl.when(j == 0)
                def _():
                    tr_send[it, r] = acc[...].astype(BF16)
                    copy.start()

        sums = []
        for r in range(groups):
            tr_copies[r].wait_recv()
            acc[...] += tr_recv[it, r].astype(F32)
            for s in range(naux):
                for k in range(size):
                    row = k * val + s * own_val
                    sum_send[it, r, s, :, k * cond:(k + 1) * cond] = acc[row:row + own_val, :].astype(BF16)
            for d in range(1, naux):
                copy = pltpu.make_async_remote_copy(
                    src_ref=sum_send.at[it, r, lax.rem(a + d, naux)], dst_ref=sum_recv.at[it, r, d],
                    send_sem=sum_ssem.at[it, r, d], recv_sem=sum_rsem.at[it, r, d],
                    device_id=peer(d, 0), device_id_type=MESH)
                copy.start()
                sums.append(copy)

        for copy in projections:
            copy.wait_recv()
        proj = proj_send[it].astype(F32)
        for da, dt in everyone:
            proj += proj_recv[it, da * ntr + dt].astype(F32)
        proj_b = proj.astype(BF16)
        for v in range(own_val):
            mixed[v] = lax.dot_general(
                proj_b, pair[v], (((1,), (1,)), ((), ())), preferred_element_type=F32)
        for copy in sums:
            copy.wait_recv()
        result = []
        for r in range(groups):
            total = sum_send[it, r, a].astype(F32)
            for d in range(1, naux):
                total += sum_recv[it, r, d].astype(F32)
            for k in range(size):
                n = r * size + k
                result.append(gap * x[n] + total[:, k * cond:(k + 1) * cond] + mixed[:, n, :])
        for copy in [c for part in gathers for c in part] + projections + sums + tr_copies:
            copy.wait_send()
        return result

    first = apply(0, [trial_k[g * half + k] for k in range(half)])

    trial = trial_k[...]
    lanes = lax.broadcasted_iota(jnp.int32, (vectors, 128), 1)
    partial = jnp.zeros((vectors, 128), F32)
    for j in range(half):
        lanewise = jnp.sum(trial * first[j][None], axis=1)
        column = jnp.sum(lanewise, axis=1, keepdims=True)
        partial += jnp.where(lanes == g * half + j, column, 0.0)
    dots_send[0] = partial
    dots = to_all(0, dots_send, dots_recv, dots_ssem, dots_rsem)
    for copy in dots:
        copy.start()
    for copy in dots:
        copy.wait()
    for da, dt in everyone:
        partial += dots_recv[0, da * ntr + dt]
    inter = partial / (naux * own_val * ntr * cond)
    dots_send[1] = inter
    core_dots = pltpu.make_async_remote_copy(
        src_ref=dots_send.at[1], dst_ref=core_recv,
        send_sem=core_ssem.at[0], recv_sem=core_rsem.at[0],
        device_id={"grp": 1 - g}, device_id_type=MESH)
    core_dots.start()

    correction = []
    for j in range(half):
        column = jnp.sum(jnp.where(lanes == g * half + j, inter, 0.0), axis=1, keepdims=True)
        fitted = trial_k[0] * column[0:1, :]
        for k in range(1, vectors):
            fitted += trial_k[k] * column[k:k + 1, :]
        correction.append((first[j] - fitted) / gap)

    second = apply(1, correction)
    for k in range(half):
        final_send[k] = second[k]
        out_ref[g * half + k] = second[k]
    final_copy = pltpu.make_async_remote_copy(
        src_ref=final_send, dst_ref=final_recv,
        send_sem=core_ssem.at[1], recv_sem=core_rsem.at[1],
        device_id={"grp": 1 - g}, device_id_type=MESH)
    final_copy.start()
    core_dots.wait()
    inter_ref[...] = (dots_send[1] + core_recv[...])[:, :vectors]
    final_copy.wait()
    for k in range(half):
        out_ref[(1 - g) * half + k] = final_recv[k]


def finish(applied_ref, inter_ref, out_ref, inter_out_ref):
    for k in range(applied_ref.shape[0]):
        out_ref[:, k, :] = applied_ref[k]
    inter_out_ref[...] = inter_ref[...]


def body(naux, ntr, trial_vectors, energy_val, energy_cond, coef_occ, coef_virt, pair_coef, live_aux):
    own_val, vectors, cond = trial_vectors.shape
    slots, val, _ = coef_occ.shape
    naux_all = pair_coef.shape[2]
    half = vectors // 2
    groups = GROUPS
    size = half // groups
    peers = naux * ntr
    vmem = pl.BlockSpec(memory_space=pltpu.VMEM)
    hbm = pl.BlockSpec(memory_space=pl.ANY)
    dma = pltpu.SemaphoreType.DMA
    scratch = [
        pltpu.VMEM(coef_occ.shape, BF16),
        pltpu.VMEM(coef_virt.shape, BF16),
        pltpu.VMEM(pair_coef.shape, BF16),
        pltpu.VMEM((groups, slots // CHUNK, size * val, CHUNK * cond), BF16),
        pltpu.VMEM((size * val, cond), F32),
        pltpu.VMEM((val, size * cond), F32),
        pltpu.VMEM((own_val, half, cond), F32),
        pltpu.VMEM((vectors, own_val, cond), F32),
        pltpu.VMEM((2, groups, own_val, size * cond), BF16),
        pltpu.VMEM((2, groups, naux, own_val, size * cond), BF16),
        pltpu.VMEM((2, half, naux_all), BF16),
        pltpu.VMEM((2, peers, half, naux_all), BF16),
        pltpu.VMEM((2, groups, size * val, cond), BF16),
        pltpu.VMEM((2, groups, size * val, cond), BF16),
        pltpu.VMEM((2, groups, naux, own_val, size * cond), BF16),
        pltpu.VMEM((2, groups, naux, own_val, size * cond), BF16),
        pltpu.VMEM((2, vectors, 128), F32),
        pltpu.VMEM((1, peers, vectors, 128), F32),
        pltpu.VMEM((vectors, 128), F32),
        pltpu.VMEM((half, own_val, cond), F32),
        pltpu.VMEM((half, own_val, cond), F32),
        dma((3,)),
        dma((2, groups, naux)), dma((2, groups, naux)),
        dma((2, peers)), dma((2, peers)),
        dma((2, groups)), dma((2, groups)),
        dma((2, groups, naux)), dma((2, groups, naux)),
        dma((1, peers)), dma((1, peers)),
        dma((2,)), dma((2,)),
    ]
    applied, intersection = pl.pallas_call(
        functools.partial(kernel, naux, ntr, groups),
        out_shape=(
            jax.ShapeDtypeStruct((vectors, own_val, cond), F32),
            jax.ShapeDtypeStruct((vectors, vectors), F32),
        ),
        in_specs=[vmem, vmem, vmem, vmem, hbm, hbm, hbm],
        out_specs=(vmem, vmem),
        scratch_shapes=scratch,
        compiler_params=pltpu.CompilerParams(
            collective_id=0, has_side_effects=True, vmem_limit_bytes=56 * 1024 * 1024
        ),
    )(
        live_aux.reshape(1, 1), trial_vectors, energy_val.reshape(1, -1),
        energy_cond.reshape(1, -1), coef_occ, coef_virt, pair_coef,
    )
    return pl.pallas_call(
        finish,
        out_shape=(
            jax.ShapeDtypeStruct(trial_vectors.shape, F32),
            jax.ShapeDtypeStruct((vectors, vectors), F32),
        ),
        in_specs=[vmem, vmem],
        out_specs=(vmem, vmem),
    )(applied, intersection)


def solution(mesh):
    in_specs = (
        P("aux", None, "tr"),
        P("aux"),
        P("tr"),
        P("aux", None, None),
        P("aux", "tr", None),
        P("aux", "tr", None),
        P("aux"),
    )
    out_specs = (P("aux", None, "tr"), P())
    sizes = (mesh.shape["aux"], mesh.shape["tr"])
    return jax.shard_map(
        functools.partial(body, *sizes), mesh=mesh, in_specs=in_specs, out_specs=out_specs, check_vma=False
    )
```
